32 devices in a mesh: seq: 16 (over z, y, x), head: 2 (over core).
Axes of the slice: x: 2, y: 2, z: 4, core: 2. Of those that a mesh axis runs over, the one named last changes fastest.
Arguments:
- queries: bfloat16 [2048, 32, 128], P('seq', 'head'), may hold values from -240 to 240
- keys: bfloat16 [2048, 32, 128], P('seq', 'head'), may hold values from -6 to 6
- values: bfloat16 [2048, 32, 128], P('seq', 'head'), may hold values from -6 to 6
- target: bfloat16 [2048, 32, 128], P('seq', 'head'), may hold values from -6 to 6
- map_q: bfloat16 [128, 64], replicated, may hold values from -0.5 to 0.5
- map_k: bfloat16 [128, 64], replicated, may hold values from -0.5 to 0.5
Outputs:
- hybrid: bfloat16 [2048, 32, 128], P('seq', 'head')
- grad_q: float32 [128, 64], replicated
- grad_k: float32 [128, 64], replicated
The draws below stay inside these ranges and needn't reach their ends.
All inputs are finite; a program needn't handle non-finite values.
Results may differ from the reference program's by a relative error of at most 0.001.
The reference program's roundings to bfloat16 on the way (of `phi_q`, `phi_k`, `far_grad` and `state_grad`) count: a program that leaves them out, or rounds other values in their place, can miss the bound.
Values may be sent and summed in bfloat16 or wider, within the bound.
No kernel may reach another device: no remote copies, remote signals or barrier semaphores. Data moves between devices by JAX's collectives and lax.ppermute only.
A program may use at most 192 MiB of HBM per device.

```python
import jax
import jax.numpy as jnp
from jax import lax

HEADS = 32
DH = 128
FEAT = 64
WINDOW = 64
TOKENS = 2048


def draw_pair(key):
    array_shape = (TOKENS, HEADS, DH)
    key_rows = jnp.clip(jax.random.normal(jax.random.fold_in(key, 101), array_shape, jnp.float32), -6.0, 6.0)
    query_rows = jnp.clip(jax.random.normal(jax.random.fold_in(key, 102), array_shape, jnp.float32), -6.0, 6.0)
    return (query_rows, key_rows)


def draw_queries(key, part):
    return draw_pair(key)[0].astype(jnp.bfloat16)


def draw_keys(key, part):
    return draw_pair(key)[1].astype(jnp.bfloat16)


def shard_levels(stream_key, dims, split, low, high):
    factor_of, own = 1.0, jax.random.fold_in(stream_key, 6)
    for position, parts in split:
        draws = jnp.exp(jax.random.uniform(jax.random.fold_in(own, position), (parts,), jnp.float32, low / len(split), high / len(split)))
        factor_of = factor_of * jnp.repeat(draws, dims[position] // parts).reshape([-1 if axis == position else 1 for axis in range(len(dims))])
    return factor_of


def gaussian(own_key, shape, spread, reach, shards=(), kind=jnp.bfloat16):
    result = spread * jax.random.normal(own_key, shape, jnp.float32)
    if shards:
        result = result * shard_levels(own_key, shape, shards, -0.22, 0.18)
    return jnp.clip(result, -reach, reach).astype(kind)


def setup_inputs(seed: int = 0) -> dict:
    key_list = jax.random.split(jax.random.key(seed), 7)
    return {
        "queries": draw_queries(jax.random.fold_in(key_list[6], 71), 0),
        "keys": draw_keys(jax.random.fold_in(key_list[6], 71), 0),
        "values": gaussian(key_list[2], (TOKENS, HEADS, DH), 1.0, 6.0, ((0, 16), (1, 2))),
        "target": gaussian(key_list[3], (TOKENS, HEADS, DH), 1.0, 6.0, ((0, 16), (1, 2))),
        "map_q": gaussian(key_list[4], (DH, FEAT), DH ** -0.5, 0.5),
        "map_k": gaussian(key_list[5], (DH, FEAT), DH ** -0.5, 0.5),
    }


highest_precision = lax.Precision.HIGHEST

def rounded(array_in):
    return lax.optimization_barrier(array_in.astype(jnp.bfloat16)).astype(jnp.float32)

def features(inputs, weight):
    hidden = jnp.einsum('thd,df->thf', inputs.astype(jnp.float32), weight.astype(jnp.float32), precision=highest_precision)
    upper_soft = jax.nn.softmax(hidden, axis=-1)
    lower_soft = jax.nn.softmax(-hidden, axis=-1)
    return (rounded(jnp.concatenate([upper_soft, lower_soft], -1)), upper_soft, lower_soft)

def feature_grad(inputs, upper_soft, lower_soft, upstream):
    feat_width = upper_soft.shape[-1]
    upper_grad = upstream[..., :feat_width]
    lower_grad = upstream[..., feat_width:]
    inner_grad = upper_soft * (upper_grad - lax.optimization_barrier(jnp.sum(upper_grad * upper_soft, -1, keepdims=True)))
    inner_grad = inner_grad - lower_soft * (lower_grad - lax.optimization_barrier(jnp.sum(lower_grad * lower_soft, -1, keepdims=True)))
    return jnp.einsum('thd,thf->df', inputs.astype(jnp.float32), rounded(inner_grad), precision=highest_precision)

def head_group(queries, keys, values, target, map_q, map_k):
    spans = TOKENS // WINDOW
    heads_here = queries.shape[1]
    phi_q, q_upper, q_lower = features(queries, map_q)
    phi_k, k_upper, k_lower = features(keys, map_k)

    def blocked(array_in):
        return array_in.reshape((spans, WINDOW) + array_in.shape[1:])

    def earlier(array_in):
        return jnp.concatenate([jnp.zeros_like(array_in[:1]), array_in[:-1]], 0)
    block_q = blocked(queries.astype(jnp.float32))
    block_k = blocked(keys.astype(jnp.float32))
    block_v = blocked(values.astype(jnp.float32))
    block_t = blocked(target.astype(jnp.float32))
    block_pq = blocked(phi_q)
    block_pk = blocked(phi_k)
    span_ids = jnp.arange(spans, dtype=jnp.int32)
    row_pos = lax.broadcasted_iota(jnp.int32, (1, WINDOW, 2 * WINDOW), 1)
    col_pos = lax.broadcasted_iota(jnp.int32, (1, WINDOW, 2 * WINDOW), 2)

    def forward(carry_in, inputs):
        states, key_sums = carry_in
        q_now, k_now, v_now, t_now, pq_now, pk_now, k_prev, v_prev, pk_prev, span_index = inputs
        near_k = jnp.concatenate([k_prev, k_now], 0)
        near_v = jnp.concatenate([v_prev, v_now], 0)
        near_p = jnp.concatenate([pk_prev, pk_now], 0)
        key_live = (span_index > 0) | (col_pos >= WINDOW)
        in_window = (col_pos > row_pos) & (col_pos <= row_pos + WINDOW) & key_live
        in_far = (col_pos <= row_pos) & key_live
        scores = jnp.einsum('thd,shd->hts', q_now, near_k, precision=highest_precision) * DH ** (-0.5)
        top_score = lax.optimization_barrier(jnp.max(jnp.where(in_window, scores, -jnp.inf), axis=-1))
        damping = jnp.exp(-top_score)
        kernel = jnp.einsum('thf,shf->hts', pq_now, near_p, precision=highest_precision)
        weight = jnp.where(in_window, jnp.exp(scores - top_score[..., None]), 0.0)
        weight = weight + jnp.where(in_far, damping[..., None] * kernel, 0.0)
        damp_rows = damping.T
        numerator = jnp.einsum('hts,shd->thd', rounded(weight), near_v, precision=highest_precision)
        numerator = numerator + damp_rows[..., None] * jnp.einsum('thf,hfd->thd', pq_now, states, precision=highest_precision)
        denominator = lax.optimization_barrier(jnp.sum(weight, -1)).T + damp_rows * jnp.einsum('thf,hf->th', pq_now, key_sums, precision=highest_precision)
        output = numerator / denominator[..., None]
        d_out = 2.0 * (output - t_now) / TOKENS
        d_numer = d_out / denominator[..., None]
        d_denom = -lax.optimization_barrier(jnp.sum(d_out * output, -1)) / denominator
        d_weight = jnp.einsum('thd,shd->hts', rounded(d_numer), near_v, precision=highest_precision) + d_denom.T[..., None]
        far_grad = rounded(jnp.where(in_far, damping[..., None] * d_weight, 0.0))
        d_phi_q = jnp.einsum('hts,shf->thf', far_grad, near_p, precision=highest_precision)
        d_phi_q = d_phi_q + damp_rows[..., None] * (jnp.einsum('thd,hfd->thf', d_numer, states, precision=highest_precision) + d_denom[..., None] * key_sums[None])
        d_near = jnp.einsum('hts,thf->shf', far_grad, pq_now, precision=highest_precision)
        state_grad = rounded(damp_rows[..., None] * d_numer)
        rate_term = damp_rows * d_denom
        states = states + jnp.einsum('shf,shd->hfd', pk_prev, v_prev, precision=highest_precision)
        key_sums = key_sums + lax.optimization_barrier(jnp.sum(pk_prev, 0))
        return ((states, key_sums), (output, d_phi_q, d_near[:WINDOW], d_near[WINDOW:], state_grad, rate_term))
    zero_state = jnp.zeros((heads_here, 2 * FEAT, DH), jnp.float32)
    zero_sum = jnp.zeros((heads_here, 2 * FEAT), jnp.float32)
    inputs_all = (block_q, block_k, block_v, block_t, block_pq, block_pk, earlier(block_k), earlier(block_v), earlier(block_pk), span_ids)
    final_carry, stacked = lax.scan(forward, (zero_state, zero_sum), inputs_all)
    outputs, d_phi_q, d_prev, d_cur, state_grads, rate_terms = stacked

    def backward(carry_in, inputs):
        near_acc, far_acc, near_sum, far_sum = carry_in
        pq_now, grad_now, rate_now, v_now = inputs
        key_grad = jnp.einsum('shd,hfd->shf', v_now, far_acc, precision=highest_precision) + far_sum[None]
        step_states = jnp.einsum('thf,thd->hfd', pq_now, grad_now, precision=highest_precision)
        step_sums = jnp.einsum('th,thf->hf', rate_now, pq_now, precision=highest_precision)
        return ((near_acc + step_states, near_acc, near_sum + step_sums, near_sum), key_grad)
    back_carry, key_grads = lax.scan(backward, (zero_state, zero_state, zero_sum, zero_sum), (block_pq, state_grads, rate_terms, block_v), reverse=True)
    d_phi_k = d_cur + jnp.concatenate([d_prev[1:], jnp.zeros_like(d_prev[:1])], 0) + key_grads
    grad_q = feature_grad(queries, q_upper, q_lower, d_phi_q.reshape(TOKENS, heads_here, 2 * FEAT))
    grad_k = feature_grad(keys, k_upper, k_lower, d_phi_k.reshape(TOKENS, heads_here, 2 * FEAT))
    return (outputs.reshape(TOKENS, heads_here, DH), grad_q, grad_k)

def reference(queries, keys, values, target, map_q, map_k):
    group_heads = 16 if HEADS % 16 == 0 else HEADS
    groups = HEADS // group_heads

    def split_heads(array_in):
        return array_in.reshape(TOKENS, groups, group_heads, DH).transpose(1, 0, 2, 3)

    def run_group(inputs):
        return head_group(inputs[0], inputs[1], inputs[2], inputs[3], map_q, map_k)
    outputs, grads_q, grads_k = lax.map(run_group, (split_heads(queries), split_heads(keys), split_heads(values), split_heads(target)))
    hybrid = outputs.transpose(1, 0, 2, 3).reshape(TOKENS, HEADS, DH).astype(jnp.bfloat16)
    return (hybrid, lax.optimization_barrier(jnp.sum(grads_q, 0)), lax.optimization_barrier(jnp.sum(grads_k, 0)))
```

```python
import functools
import math

import jax
import jax.numpy as jnp
from jax import lax
from jax.experimental import pallas as pl
from jax.experimental.pallas import tpu as pltpu
from jax.sharding import PartitionSpec as P

WINDOW = 64

F32 = jnp.float32
BF16 = jnp.bfloat16


def dot(a, b, ca, cb):
    return lax.dot_general(a, b, (((ca,), (cb,)), ((), ())), preferred_element_type=F32)


def split(x):
    hi = x.astype(BF16)
    return hi, (x - hi.astype(F32)).astype(BF16)


def half_sums(x, low):
    first = jnp.sum(jnp.where(low, x, 0.0), axis=-1, keepdims=True)
    second = jnp.sum(jnp.where(low, 0.0, x), axis=-1, keepdims=True)
    return jnp.where(low, first, second)


def half_softmax(x, low):
    first = jnp.max(jnp.where(low, x, -jnp.inf), axis=-1, keepdims=True)
    second = jnp.max(jnp.where(low, -jnp.inf, x), axis=-1, keepdims=True)
    e = jnp.exp(x - jnp.where(low, first, second))
    return e / half_sums(e, low)


def map_grad(p, d, low, feat):
    y = p * (d - half_sums(d * p, low))
    return (y - pltpu.roll(y, feat, 1)).astype(BF16)


def attend(total_tokens, x_ref, mq_ref, mk_ref, hyb_ref, grad_ref,
           kpad, vpad, ppad, soft_q, soft_k, phi_q_s, u_q, u_k, d_pad, grads, rates,
           state, ksum, tail, tail_sum):
    chunks, _, _, rows, size = x_ref.shape
    window = WINDOW
    per = rows // window
    blocks = chunks * per
    feat = size // 2
    scale = size ** (-0.5)
    head = pl.program_id(0)
    low = lax.broadcasted_iota(jnp.int32, (1, size), 1) < feat

    zero_rows = jnp.zeros((window, size), BF16)
    kpad[:window] = zero_rows
    vpad[:window] = zero_rows
    ppad[:window] = zero_rows
    d_pad[:window] = jnp.zeros((window, size), F32)
    state[...] = jnp.zeros_like(state)
    ksum[...] = jnp.zeros_like(ksum)
    tail[...] = jnp.zeros_like(tail)
    tail_sum[...] = jnp.zeros_like(tail_sum)

    @pl.when(head == 0)
    def _():
        grad_ref[...] = jnp.zeros_like(grad_ref)

    def features(i, carry):
        at = pl.ds(pl.multiple_of(i * rows, rows), rows)
        after = pl.ds(pl.multiple_of(i * rows + window, window), rows)
        q = x_ref[i, 0, 0]
        k = x_ref[i, 1, 0]
        pq = half_softmax(dot(q, mq_ref[...], 1, 0), low)
        pk = half_softmax(dot(k, mk_ref[...], 1, 0), low)
        soft_q[at] = pq
        soft_k[at] = pk
        phi_q_s[at] = pq.astype(BF16)
        ppad[after] = pk.astype(BF16)
        kpad[after] = k
        vpad[after] = x_ref[i, 2, 0]
        return carry

    lax.fori_loop(0, chunks, features, 0, unroll=False)

    row = lax.broadcasted_iota(jnp.int32, (window, 2 * window), 0)
    col = lax.broadcasted_iota(jnp.int32, (window, 2 * window), 1)

    def forward(c, chunk, part):
        inner = pl.ds(part * window, window)
        at = pl.ds(pl.multiple_of(c * window, window), window)
        after = pl.ds(pl.multiple_of(c * window + window, window), window)
        near = pl.ds(pl.multiple_of(c * window, window), 2 * window)
        q = x_ref[chunk, 0, 0, inner]
        phi = phi_q_s[at]
        near_k = kpad[near]
        near_v = vpad[near]
        near_p = ppad[near]
        first_live = jnp.where(c > 0, 0, window)
        live = col >= first_live
        in_window = (col > row) & (col <= row + window) & live
        in_far = (col <= row) & live
        scores = dot(q, near_k, 1, 1) * scale
        top = jnp.max(jnp.where(in_window, scores, -jnp.inf), axis=-1, keepdims=True)
        damp = jnp.exp(-top)
        kernel = dot(phi, near_p, 1, 1)
        weight = jnp.where(
            in_window, jnp.exp(scores - top), jnp.where(in_far, damp * kernel, 0.0)
        )
        s_hi, s_lo = split(state[...])
        sums = ksum[...]
        phi32 = phi.astype(F32)
        state_num = dot(phi, s_hi, 1, 0) + dot(phi, s_lo, 1, 0)
        state_den = jnp.sum(phi32 * sums, axis=-1, keepdims=True)
        num = dot(weight.astype(BF16), near_v, 1, 0) + damp * state_num
        den = jnp.sum(weight, axis=-1, keepdims=True) + damp * state_den
        inv = 1.0 / den
        out = num * inv
        hyb_ref[chunk, 0, inner] = out.astype(BF16)
        t = x_ref[chunk, 3, 0, inner].astype(F32)
        d_out = (out - t) * (2.0 / total_tokens)
        d_num = d_out * inv
        d_den = -jnp.sum(d_out * out, axis=-1, keepdims=True) * inv
        n_hi, n_lo = split(d_num)
        d_weight = dot(n_hi, near_v, 1, 1) + d_den
        far = jnp.where(in_far, damp * d_weight, 0.0).astype(BF16)
        d_state = dot(n_hi, s_hi, 1, 1) + (dot(n_lo, s_hi, 1, 1) + dot(n_hi, s_lo, 1, 1))
        d_phi = dot(far, near_p, 1, 0) + damp * (d_state + d_den * sums)
        u_q[at] = map_grad(soft_q[at], d_phi, low, feat)
        d_near = dot(far, phi, 0, 0)
        d_pad[at] += d_near[:window]
        d_pad[after] = d_near[window:]
        grads[c] = dot((damp * d_num).astype(BF16), phi, 0, 0)
        rates[c] = jnp.sum((damp * d_den) * phi32, axis=0, keepdims=True)
        old_p = ppad[at]
        state[...] += dot(old_p, vpad[at], 0, 0)
        ksum[...] += jnp.sum(old_p.astype(F32), axis=0, keepdims=True)

    def forward_chunk(i, carry):
        for part in range(per):
            forward(i * per + part, i, part)
        return carry

    lax.fori_loop(0, chunks, forward_chunk, 0, unroll=False)

    def backward(c):
        at = pl.ds(pl.multiple_of(c * window, window), window)
        after = pl.ds(pl.multiple_of(c * window + window, window), window)
        v = vpad[after]
        t_hi, t_lo = split(tail[...])
        d_phi = d_pad[after] + (dot(v, t_hi, 1, 0) + dot(v, t_lo, 1, 0)) + tail_sum[...]
        u_k[at] = map_grad(soft_k[at], d_phi, low, feat)
        later = jnp.minimum(c + 1, blocks - 1)
        fresh = c + 1 < blocks
        tail[...] += jnp.where(fresh, grads[later], 0.0)
        tail_sum[...] += jnp.where(fresh, rates[later], 0.0)

    def backward_chunk(i, carry):
        for part in range(per):
            backward(blocks - 1 - (i * per + part))
        return carry

    lax.fori_loop(0, chunks, backward_chunk, 0, unroll=False)

    def reduce_chunk(i, carry):
        at = pl.ds(pl.multiple_of(i * rows, rows), rows)
        gq = dot(x_ref[i, 0, 0], u_q[at], 0, 0)
        gk = dot(x_ref[i, 1, 0], u_k[at], 0, 0)
        grad_ref[...] += jnp.where(low, gq, -gk)
        return carry

    lax.fori_loop(0, chunks, reduce_chunk, 0, unroll=False)


def attend_call(x, map_q, map_k, total_tokens):
    chunks, four, heads, rows, size = x.shape
    tokens = chunks * rows
    blocks = tokens // WINDOW
    vmem = pltpu.VMEM
    return pl.pallas_call(
        functools.partial(attend, total_tokens),
        grid=(heads,),
        in_specs=[
            pl.BlockSpec((chunks, four, 1, rows, size), lambda h: (0, 0, h, 0, 0)),
            pl.BlockSpec((size, size), lambda h: (0, 0)),
            pl.BlockSpec((size, size), lambda h: (0, 0)),
        ],
        out_specs=[
            pl.BlockSpec((chunks, 1, rows, size), lambda h: (0, h, 0, 0)),
            pl.BlockSpec((size, size), lambda h: (0, 0)),
        ],
        out_shape=[
            jax.ShapeDtypeStruct((chunks, heads, rows, size), BF16),
            jax.ShapeDtypeStruct((size, size), F32),
        ],
        scratch_shapes=[
            vmem((tokens + WINDOW, size), BF16),
            vmem((tokens + WINDOW, size), BF16),
            vmem((tokens + WINDOW, size), BF16),
            vmem((tokens, size), F32),
            vmem((tokens, size), F32),
            vmem((tokens, size), BF16),
            vmem((tokens, size), BF16),
            vmem((tokens, size), BF16),
            vmem((tokens + WINDOW, size), F32),
            vmem((blocks, size, size), F32),
            vmem((blocks, 1, size), F32),
            vmem((size, size), F32),
            vmem((1, size), F32),
            vmem((size, size), F32),
            vmem((1, size), F32),
        ],
        name="attend",
    )(x, map_q, map_k)


def swap_sum(value, axis, count, bit):
    return value + lax.ppermute(value, axis, [(i, i ^ bit) for i in range(count)])


def sum_everywhere(value):
    for axis in ("head", "seq"):
        count = lax.axis_size(axis)
        if count & (count - 1):
            value = lax.psum(value, axis)
            continue
        bit = 1
        while bit < count:
            value = swap_sum(value, axis, count, bit)
            bit *= 2
    return value


def per_device(queries, keys, values, target, map_q, map_k):
    rows, heads, size = queries.shape
    seq_count = lax.axis_size("seq")
    here = lax.axis_index("seq")
    total_tokens = rows * seq_count
    group = math.gcd(seq_count, heads)
    groups = seq_count // group
    own_heads = heads // group
    members = [list(range(g * group, (g + 1) * group)) for g in range(groups)]

    def trade(array):
        if group == 1:
            return array
        return lax.all_to_all(array, "seq", 0, 0, axis_index_groups=members)

    stacked = jnp.stack([queries, keys, values, target], 0)
    stacked = stacked.reshape(4, rows, group, own_heads, size).transpose(2, 0, 3, 1, 4)
    x = trade(stacked)
    if groups > 1:
        across = [[g * group + m for g in range(groups)] for m in range(group)]
        x = lax.all_gather(x, "seq", axis_index_groups=across)
        x = x.reshape((groups * group,) + x.shape[2:])

    both_q = jnp.concatenate([map_q, -map_q], 1)
    both_k = jnp.concatenate([map_k, -map_k], 1)
    hyb, grad = attend_call(x, both_q, both_k, total_tokens)
    if groups > 1:
        mine = here // group
        hyb = lax.dynamic_slice_in_dim(hyb, mine * group, group, 0)
        grad = jnp.where(mine == 0, grad, 0.0)
    hybrid = trade(hyb).transpose(2, 0, 1, 3).reshape(rows, heads, size)
    grad = sum_everywhere(grad)
    feat = map_q.shape[1]
    return hybrid, grad[:, :feat], grad[:, feat:]


def solution(mesh):
    tokens = P("seq", "head", None)
    return jax.shard_map(
        per_device,
        mesh=mesh,
        in_specs=(tokens, tokens, tokens, tokens, P(), P()),
        out_specs=(tokens, P(), P()),
        check_vma=False,
    )
```

```python
import functools
import math

import jax
import jax.numpy as jnp
from jax import lax
from jax.experimental import pallas as pl
from jax.experimental.pallas import tpu as pltpu
from jax.sharding import PartitionSpec as P

WINDOW = 64

F32 = jnp.float32
BF16 = jnp.bfloat16

FEATURE_CHUNKS = 8
FORWARD_CHUNKS = 4
BACK_BLOCKS = 16
SUM_CHUNKS = 16


def dot(a, b, ca, cb):
    return lax.dot_general(a, b, (((ca,), (cb,)), ((), ())), preferred_element_type=F32)


def split(x):
    hi = x.astype(BF16)
    return hi, (x - hi.astype(F32)).astype(BF16)


def half_sums(xs, low):
    first = [jnp.sum(jnp.where(low, x, 0.0), axis=-1, keepdims=True) for x in xs]
    second = [jnp.sum(jnp.where(low, 0.0, x), axis=-1, keepdims=True) for x in xs]
    return [jnp.where(low, a, b) for a, b in zip(first, second)]


def half_softmax(xs, low):
    first = [jnp.max(jnp.where(low, x, -jnp.inf), axis=-1, keepdims=True) for x in xs]
    second = [jnp.max(jnp.where(low, -jnp.inf, x), axis=-1, keepdims=True) for x in xs]
    es = [jnp.exp(x - jnp.where(low, a, b)) for x, a, b in zip(xs, first, second)]
    return [e / total for e, total in zip(es, half_sums(es, low))]


def map_grad(ps, ds, low, feat):
    means = half_sums([d * p for p, d in zip(ps, ds)], low)
    ys = [p * (d - mean) for p, d, mean in zip(ps, ds, means)]
    return [(y - pltpu.roll(y, feat, 1)).astype(BF16) for y in ys]


def attend(total_tokens, x_ref, mq_ref, mk_ref, hyb_ref, grad_ref,
           kpad, vpad, ppad, soft_q, soft_k, phi_q_s, u_q, u_k, d_pad, grads, rates,
           state, ksum, tail, tail_sum):
    chunks, _, _, rows, size = x_ref.shape
    window = WINDOW
    per = rows // window
    blocks = chunks * per
    feat = size // 2
    scale = size ** (-0.5)
    head = pl.program_id(0)
    low = lax.broadcasted_iota(jnp.int32, (1, size), 1) < feat

    zero_rows = jnp.zeros((window, size), BF16)
    kpad[:window] = zero_rows
    vpad[:window] = zero_rows
    ppad[:window] = zero_rows
    d_pad[:window] = jnp.zeros((window, size), F32)
    state[...] = jnp.zeros_like(state)
    ksum[...] = jnp.zeros_like(ksum)
    tail[...] = jnp.zeros_like(tail)
    tail_sum[...] = jnp.zeros_like(tail_sum)

    @pl.when(head == 0)
    def _():
        grad_ref[...] = jnp.zeros_like(grad_ref)

    feature_chunks = math.gcd(chunks, FEATURE_CHUNKS)

    def features(i, carry):
        steps = range(feature_chunks)
        at = [pl.ds(pl.multiple_of((i * feature_chunks + j) * rows, rows), rows) for j in steps]
        after = [
            pl.ds(pl.multiple_of((i * feature_chunks + j) * rows + window, window), rows)
            for j in steps
        ]
        q = [x_ref[i * feature_chunks + j, 0, 0] for j in steps]
        k = [x_ref[i * feature_chunks + j, 1, 0] for j in steps]
        pq = half_softmax([dot(x, mq_ref[...], 1, 0) for x in q], low)
        pk = half_softmax([dot(x, mk_ref[...], 1, 0) for x in k], low)
        for j in steps:
            soft_q[at[j]] = pq[j]
            soft_k[at[j]] = pk[j]
            phi_q_s[at[j]] = pq[j].astype(BF16)
            ppad[after[j]] = pk[j].astype(BF16)
            kpad[after[j]] = k[j]
            vpad[after[j]] = x_ref[i * feature_chunks + j, 2, 0]
        return carry

    lax.fori_loop(0, chunks // feature_chunks, features, 0)

    row = lax.broadcasted_iota(jnp.int32, (window, 2 * window), 0)
    col = lax.broadcasted_iota(jnp.int32, (window, 2 * window), 1)

    forward_chunks = math.gcd(chunks, FORWARD_CHUNKS)
    batch = forward_chunks * per

    def forward(i, carry):
        steps = range(batch)
        c = [i * batch + j for j in steps]
        x_at = [(i * forward_chunks + j // per, pl.ds(j % per * window, window)) for j in steps]
        at = [pl.ds(pl.multiple_of(cj * window, window), window) for cj in c]
        near = [pl.ds(pl.multiple_of(cj * window, window), 2 * window) for cj in c]
        q = [x_ref[x_at[j][0], 0, 0, x_at[j][1]] for j in steps]
        phi = [phi_q_s[at[j]] for j in steps]
        near_k = [kpad[near[j]] for j in steps]
        near_v = [vpad[near[j]] for j in steps]
        near_p = [ppad[near[j]] for j in steps]
        live = col >= jnp.where(i > 0, 0, window)
        in_window = [(col > row) & (col <= row + window)] * batch
        in_far = [col <= row] * batch
        in_window[0] = in_window[0] & live
        in_far[0] = in_far[0] & live
        scores = [dot(q[j], near_k[j], 1, 1) * scale for j in steps]
        kernel = [dot(phi[j], near_p[j], 1, 1) for j in steps]
        fresh = [dot(near_p[j][:window], near_v[j][:window], 0, 0) for j in steps]
        fresh_sum = [
            jnp.sum(near_p[j][:window].astype(F32), axis=0, keepdims=True) for j in steps
        ]
        states = [state[...]]
        sums = [ksum[...]]
        for j in steps:
            states.append(states[-1] + fresh[j])
            sums.append(sums[-1] + fresh_sum[j])
        state[...] = states[-1]
        ksum[...] = sums[-1]
        s_hi, s_lo = zip(*[split(states[j]) for j in steps])
        phi32 = [phi[j].astype(F32) for j in steps]
        state_num = [dot(phi[j], s_hi[j], 1, 0) + dot(phi[j], s_lo[j], 1, 0) for j in steps]
        state_den = [jnp.sum(phi32[j] * sums[j], axis=-1, keepdims=True) for j in steps]
        top = [
            jnp.max(jnp.where(in_window[j], scores[j], -jnp.inf), axis=-1, keepdims=True)
            for j in steps
        ]
        damp = [jnp.exp(-top[j]) for j in steps]
        weight = [
            jnp.where(
                in_window[j],
                jnp.exp(scores[j] - top[j]),
                jnp.where(in_far[j], damp[j] * kernel[j], 0.0),
            )
            for j in steps
        ]
        num = [dot(weight[j].astype(BF16), near_v[j], 1, 0) + damp[j] * state_num[j] for j in steps]
        inv = [
            1.0 / (jnp.sum(weight[j], axis=-1, keepdims=True) + damp[j] * state_den[j])
            for j in steps
        ]
        out = [num[j] * inv[j] for j in steps]
        for j in steps:
            hyb_ref[x_at[j][0], 0, x_at[j][1]] = out[j].astype(BF16)
        t = [x_ref[x_at[j][0], 3, 0, x_at[j][1]].astype(F32) for j in steps]
        d_out = [(out[j] - t[j]) * (2.0 / total_tokens) for j in steps]
        d_num = [d_out[j] * inv[j] for j in steps]
        d_den = [-jnp.sum(d_out[j] * out[j], axis=-1, keepdims=True) * inv[j] for j in steps]
        n_hi, n_lo = zip(*[split(d_num[j]) for j in steps])
        d_weight = [dot(n_hi[j], near_v[j], 1, 1) + d_den[j] for j in steps]
        d_state = [
            dot(n_hi[j], s_hi[j], 1, 1)
            + (dot(n_lo[j], s_hi[j], 1, 1) + dot(n_hi[j], s_lo[j], 1, 1))
            for j in steps
        ]
        far = [jnp.where(in_far[j], damp[j] * d_weight[j], 0.0).astype(BF16) for j in steps]
        d_phi = [
            dot(far[j], near_p[j], 1, 0) + damp[j] * (d_state[j] + d_den[j] * sums[j])
            for j in steps
        ]
        for j in steps:
            grads[c[j]] = dot((damp[j] * d_num[j]).astype(BF16), phi[j], 0, 0)
            rates[c[j]] = jnp.sum((damp[j] * d_den[j]) * phi32[j], axis=0, keepdims=True)
        d_near = [dot(far[j], phi[j], 0, 0) for j in steps]
        d_pad[at[0]] += d_near[0][:window]
        for j in steps[1:]:
            d_pad[at[j]] = d_near[j - 1][window:] + d_near[j][:window]
        last = pl.ds(pl.multiple_of((i * batch + batch) * window, window), window)
        d_pad[last] = d_near[-1][window:]
        u = map_grad([soft_q[at[j]] for j in steps], d_phi, low, feat)
        for j in steps:
            u_q[at[j]] = u[j]
        return carry

    lax.fori_loop(0, blocks // batch, forward, 0)

    back_batch = math.gcd(blocks, BACK_BLOCKS)

    def backward(i, carry):
        steps = range(back_batch)
        c = [blocks - 1 - (i * back_batch + j) for j in steps]
        at = [pl.ds(pl.multiple_of(cj * window, window), window) for cj in c]
        after = [pl.ds(pl.multiple_of(cj * window + window, window), window) for cj in c]
        tails = [tail[...]]
        tail_sums = [tail_sum[...]]
        for j in steps:
            if j == 0:
                later = jnp.minimum(c[0] + 1, blocks - 1)
                here = i > 0
                tails.append(tails[-1] + jnp.where(here, grads[later], 0.0))
                tail_sums.append(tail_sums[-1] + jnp.where(here, rates[later], 0.0))
            else:
                tails.append(tails[-1] + grads[c[j] + 1])
                tail_sums.append(tail_sums[-1] + rates[c[j] + 1])
        tail[...] = tails[-1]
        tail_sum[...] = tail_sums[-1]
        v = [vpad[after[j]] for j in steps]
        t_hi, t_lo = zip(*[split(tails[j]) for j in steps])
        d_phi = [
            d_pad[after[j]]
            + (dot(v[j], t_hi[j], 1, 0) + dot(v[j], t_lo[j], 1, 0))
            + tail_sums[j]
            for j in steps
        ]
        u = map_grad([soft_k[at[j]] for j in steps], d_phi, low, feat)
        for j in steps:
            u_k[at[j]] = u[j]
        return carry

    lax.fori_loop(0, blocks // back_batch, backward, 0)

    sum_chunks = math.gcd(chunks, SUM_CHUNKS)
    length = sum_chunks * rows

    def total(i, carry):
        at = pl.ds(pl.multiple_of(i * length, length), length)
        mine = pl.ds(i * sum_chunks, sum_chunks)
        gq = dot(x_ref[mine, 0, 0].reshape(length, size), u_q[at], 0, 0)
        gk = dot(x_ref[mine, 1, 0].reshape(length, size), u_k[at], 0, 0)
        grad_ref[...] += jnp.where(low, gq, -gk)
        return carry

    lax.fori_loop(0, chunks // sum_chunks, total, 0)


def attend_call(x, map_q, map_k, total_tokens):
    chunks, four, heads, rows, size = x.shape
    tokens = chunks * rows
    blocks = tokens // WINDOW
    vmem = pltpu.VMEM
    return pl.pallas_call(
        functools.partial(attend, total_tokens),
        grid=(heads,),
        in_specs=[
            pl.BlockSpec((chunks, four, 1, rows, size), lambda h: (0, 0, h, 0, 0)),
            pl.BlockSpec((size, size), lambda h: (0, 0)),
            pl.BlockSpec((size, size), lambda h: (0, 0)),
        ],
        out_specs=[
            pl.BlockSpec((chunks, 1, rows, size), lambda h: (0, h, 0, 0)),
            pl.BlockSpec((size, size), lambda h: (0, 0)),
        ],
        out_shape=[
            jax.ShapeDtypeStruct((chunks, heads, rows, size), BF16),
            jax.ShapeDtypeStruct((size, size), F32),
        ],
        scratch_shapes=[
            vmem((tokens + WINDOW, size), BF16),
            vmem((tokens + WINDOW, size), BF16),
            vmem((tokens + WINDOW, size), BF16),
            vmem((tokens, size), F32),
            vmem((tokens, size), F32),
            vmem((tokens, size), BF16),
            vmem((tokens, size), BF16),
            vmem((tokens, size), BF16),
            vmem((tokens + WINDOW, size), F32),
            vmem((blocks, size, size), F32),
            vmem((blocks, 1, size), F32),
            vmem((size, size), F32),
            vmem((1, size), F32),
            vmem((size, size), F32),
            vmem((1, size), F32),
        ],
        name="attend",
    )(x, map_q, map_k)


def sum_everywhere(value):
    def partner(axis, count, bits):
        return lax.ppermute(value, axis, [(i, i ^ bits) for i in range(count)])

    for axis in ("head", "seq"):
        count = lax.axis_size(axis)
        if count & (count - 1):
            value = lax.psum(value, axis)
            continue
        bit = 1
        while bit < count:
            if 2 * bit < count:
                one, two, three = (partner(axis, count, m * bit) for m in (1, 2, 3))
                value = (value + one) + (two + three)
                bit *= 4
            else:
                value = value + partner(axis, count, bit)
                bit *= 2
    return value


def per_device(queries, keys, values, target, map_q, map_k):
    rows, heads, size = queries.shape
    seq_count = lax.axis_size("seq")
    here = lax.axis_index("seq")
    total_tokens = rows * seq_count
    group = math.gcd(seq_count, heads)
    groups = seq_count // group
    own_heads = heads // group
    members = [list(range(g * group, (g + 1) * group)) for g in range(groups)]

    def trade(array):
        if group == 1:
            return array
        return lax.all_to_all(array, "seq", 0, 0, axis_index_groups=members)

    stacked = jnp.stack([queries, keys, values, target], 0)
    stacked = stacked.reshape(4, rows, group, own_heads, size).transpose(2, 0, 3, 1, 4)
    x = trade(stacked)
    if groups > 1:
        across = [[g * group + m for g in range(groups)] for m in range(group)]
        x = lax.all_gather(x, "seq", axis_index_groups=across)
        x = x.reshape((groups * group,) + x.shape[2:])

    both_q = jnp.concatenate([map_q, -map_q], 1)
    both_k = jnp.concatenate([map_k, -map_k], 1)
    hyb, grad = attend_call(x, both_q, both_k, total_tokens)
    if groups > 1:
        mine = here // group
        hyb = lax.dynamic_slice_in_dim(hyb, mine * group, group, 0)
        grad = jnp.where(mine == 0, grad, 0.0)
    hybrid = trade(hyb).transpose(2, 0, 1, 3).reshape(rows, heads, size)
    grad = sum_everywhere(grad)
    feat = map_q.shape[1]
    return hybrid, grad[:, :feat], grad[:, feat:]


def solution(mesh):
    tokens = P("seq", "head", None)
    return jax.shard_map(
        per_device,
        mesh=mesh,
        in_specs=(tokens, tokens, tokens, tokens, P(), P()),
        out_specs=(tokens, P(), P()),
        check_vma=False,
    )
```

```python
import functools
import math

import jax
import jax.numpy as jnp
from jax import lax
from jax.experimental import pallas as pl
from jax.experimental.pallas import tpu as pltpu
from jax.sharding import PartitionSpec as P

WINDOW = 64

F32 = jnp.float32
BF16 = jnp.bfloat16

FEATURE_CHUNKS = 8
FORWARD_CHUNKS = 4
BACK_BLOCKS = 16
SUM_CHUNKS = 16
DEAL_ROWS = 32
KERNEL_VMEM = 16 << 20


def dot(a, b, ca, cb):
    return lax.dot_general(a, b, (((ca,), (cb,)), ((), ())), preferred_element_type=F32)


def split(x):
    hi = x.astype(BF16)
    return hi, (x - hi.astype(F32)).astype(BF16)


def half_sums(xs, ones):
    sums = []
    for x in xs:
        hi = x.astype(BF16)
        rest = x - hi.astype(F32)
        mid, low = split(rest)
        sums.append(dot(jnp.concatenate([hi, mid], 1), ones, 1, 0) + dot(low, ones[: x.shape[1]], 1, 0))
    return sums


def half_ones(size):
    row = lax.broadcasted_iota(jnp.int32, (2 * size, size), 0)
    col = lax.broadcasted_iota(jnp.int32, (2 * size, size), 1)
    half = size // 2
    return jnp.where((row // half) % 2 == col // half, 1.0, 0.0).astype(BF16)


def in_vmem(*arrays):
    return [pltpu.with_memory_space_constraint(array, pltpu.VMEM) for array in arrays]


def resident(kernel, outs, scratch, *args, smem=0, name):
    vmem = pl.BlockSpec(memory_space=pltpu.VMEM)
    scalar = pl.BlockSpec(memory_space=pltpu.SMEM)
    return pl.pallas_call(
        kernel,
        in_specs=[scalar] * smem + [vmem] * (len(args) - smem),
        out_specs=[vmem] * len(outs),
        out_shape=outs,
        scratch_shapes=scratch,
        compiler_params=pltpu.CompilerParams(vmem_limit_bytes=KERNEL_VMEM),
        name=name,
    )(*args[:smem], *in_vmem(*args[smem:]))


def half_softmax(xs, ones):
    low = lax.broadcasted_iota(jnp.int32, (1, xs[0].shape[1]), 1) < xs[0].shape[1] // 2
    first = [jnp.max(jnp.where(low, x, -jnp.inf), axis=-1, keepdims=True) for x in xs]
    second = [jnp.max(jnp.where(low, -jnp.inf, x), axis=-1, keepdims=True) for x in xs]
    es = [jnp.exp(x - jnp.where(low, a, b)) for x, a, b in zip(xs, first, second)]
    return [e / total for e, total in zip(es, half_sums(es, ones))]


def map_grad(ps, ds, ones):
    means = half_sums([d * p for p, d in zip(ps, ds)], ones)
    ys = [p * (d - mean) for p, d, mean in zip(ps, ds, means)]
    return [(y - pltpu.roll(y, y.shape[1] // 2, 1)).astype(BF16) for y in ys]


def over_heads(heads):
    return lambda body: lax.fori_loop(0, heads, lambda h, carry: body(h) or carry, 0)


def key_states(x_ref, mk_ref, sums_ref, last_ref, halo_ref, phi_s):
    chunks, _, heads, rows, size = x_ref.shape
    window = WINDOW
    tokens = chunks * rows
    ones = half_ones(size)
    batch = math.gcd(chunks, FEATURE_CHUNKS)
    length = batch * rows
    sums_ref[...] = jnp.zeros_like(sums_ref)
    last_ref[...] = jnp.zeros_like(last_ref)

    @over_heads(heads)
    def _(h):
        def features(i, carry):
            steps = range(batch)
            soft = half_softmax(
                [dot(x_ref[i * batch + j, 0, h], mk_ref[...], 1, 1) for j in steps], ones
            )
            phi = jnp.concatenate(soft, 0).astype(BF16)
            phi_s[...] = phi
            at = i * length + lax.broadcasted_iota(jnp.int32, (length, size), 0)
            early = jnp.where(at < tokens - window, phi.astype(F32), 0.0)
            v = x_ref[pl.ds(i * batch, batch), 1, h].reshape(length, size)
            sums_ref[h, :size] += dot(early.astype(BF16), v, 0, 0)
            sums_ref[h, size : size + 1] += jnp.sum(early, axis=0, keepdims=True)
            return carry

        lax.fori_loop(0, chunks // batch, features, 0)
        phi_last = phi_s[length - window :]
        k_last = x_ref[chunks - 1, 0, h, rows - window :]
        v_last = x_ref[chunks - 1, 1, h, rows - window :]
        last_ref[h, :size] = dot(phi_last, v_last, 0, 0)
        last_ref[h, size : size + 1] = jnp.sum(phi_last.astype(F32), axis=0, keepdims=True)
        halo_ref[0, h] = k_last
        halo_ref[1, h] = v_last


def key_states_call(x, map_k):
    chunks, _, heads, rows, size = x.shape
    batch = math.gcd(chunks, FEATURE_CHUNKS)
    state = jax.ShapeDtypeStruct((heads, size + 8, size), F32)
    return resident(
        key_states,
        [state, state, jax.ShapeDtypeStruct((2, heads, WINDOW, size), BF16)],
        [pltpu.VMEM((batch * rows, size), BF16)],
        x,
        map_k,
        name="key_states",
    )


def feature_maps(x_ref, mk_ref, mq_ref, soft_k, soft_q, phi_k, phi_q):
    chunks, _, heads, rows, size = x_ref.shape
    ones = half_ones(size)
    batch = math.gcd(chunks, FEATURE_CHUNKS)

    @over_heads(heads)
    def _(h):
        def features(i, carry):
            steps = range(batch)
            at = [pl.ds(pl.multiple_of((i * batch + j) * rows, rows), rows) for j in steps]
            for which, m_ref, soft, phi in (
                (0, mk_ref, soft_k, phi_k),
                (2, mq_ref, soft_q, phi_q),
            ):
                p = half_softmax(
                    [dot(x_ref[i * batch + j, which, h], m_ref[...], 1, 1) for j in steps], ones
                )
                for j in steps:
                    soft[h, at[j]] = p[j]
                    phi[h, at[j]] = p[j].astype(BF16)
            return carry

        lax.fori_loop(0, chunks // batch, features, 0)


def feature_maps_call(x, map_k, map_q):
    chunks, _, heads, rows, size = x.shape
    wide = pltpu.VMEM((heads, chunks * rows, size), F32)
    narrow = pltpu.VMEM((heads, chunks * rows, size), BF16)
    return resident(
        feature_maps, [wide, wide, narrow, narrow], [], x, map_k, map_q, name="feature_maps"
    )


def attend(total_tokens, live_ref, x_ref, halo_ref, prior_ref, mk_ref, phi_k, phi_q,
           hyb_ref, send_ref, d_q, d_pad, grads, rates,
           kpad, vpad, ppad, state, ksum, all_grads, all_rates):
    chunks, _, heads, rows, size = x_ref.shape
    window = WINDOW
    per = rows // window
    blocks = chunks * per
    tokens = chunks * rows
    scale = size ** (-0.5)
    ones = half_ones(size)
    has_prior = live_ref[0] > 0

    row = lax.broadcasted_iota(jnp.int32, (window, 2 * window), 0)
    col = lax.broadcasted_iota(jnp.int32, (window, 2 * window), 1)

    forward_chunks = math.gcd(chunks, FORWARD_CHUNKS)
    batch = forward_chunks * per

    @over_heads(heads)
    def _(h):
        kpad[:window] = halo_ref[0, h]
        vpad[:window] = halo_ref[1, h]
        (soft_halo,) = half_softmax([dot(halo_ref[0, h], mk_ref[...], 1, 1)], ones)
        ppad[:window] = jnp.where(has_prior, soft_halo, 0.0).astype(BF16)
        ppad[window:] = phi_k[h]
        kpad[window:] = x_ref[:, 0, h].reshape(tokens, size)
        vpad[window:] = x_ref[:, 1, h].reshape(tokens, size)
        state[...] = prior_ref[h, :size]
        ksum[...] = prior_ref[h, size : size + 1]
        all_grads[...] = jnp.zeros_like(all_grads)
        all_rates[...] = jnp.zeros_like(all_rates)
        d_pad[h, :window] = jnp.zeros((window, size), F32)

        def forward(i, carry):
            steps = range(batch)
            c = [i * batch + j for j in steps]
            x_at = [(i * forward_chunks + j // per, pl.ds(j % per * window, window)) for j in steps]
            at = [pl.ds(pl.multiple_of(cj * window, window), window) for cj in c]
            near = [pl.ds(pl.multiple_of(cj * window, window), 2 * window) for cj in c]
            q = [x_ref[x_at[j][0], 2, h, x_at[j][1]] for j in steps]
            phi = [phi_q[h, at[j]] for j in steps]
            near_k = [kpad[near[j]] for j in steps]
            near_v = [vpad[near[j]] for j in steps]
            near_p = [ppad[near[j]] for j in steps]
            live = col >= jnp.where((i > 0) | has_prior, 0, window)
            in_window = [(col > row) & (col <= row + window)] * batch
            in_far = [col <= row] * batch
            in_window[0] = in_window[0] & live
            in_far[0] = in_far[0] & live
            scores = [dot(q[j], near_k[j], 1, 1) * scale for j in steps]
            kernel = [dot(phi[j], near_p[j], 1, 1) for j in steps]
            fresh = [dot(near_p[j][:window], near_v[j][:window], 0, 0) for j in steps]
            fresh_sum = [
                jnp.sum(near_p[j][:window].astype(F32), axis=0, keepdims=True) for j in steps
            ]
            states = [state[...]]
            sums = [ksum[...]]
            for j in steps:
                states.append(states[-1] + fresh[j])
                sums.append(sums[-1] + fresh_sum[j])
            state[...] = states[-1]
            ksum[...] = sums[-1]
            s_hi, s_lo = zip(*[split(states[j]) for j in steps])
            phi32 = [phi[j].astype(F32) for j in steps]
            state_num = [dot(phi[j], s_hi[j], 1, 0) + dot(phi[j], s_lo[j], 1, 0) for j in steps]
            state_den = [jnp.sum(phi32[j] * sums[j], axis=-1, keepdims=True) for j in steps]
            top = [
                jnp.max(jnp.where(in_window[j], scores[j], -jnp.inf), axis=-1, keepdims=True)
                for j in steps
            ]
            damp = [jnp.exp(-top[j]) for j in steps]
            weight = [
                jnp.where(
                    in_window[j],
                    jnp.exp(scores[j] - top[j]),
                    jnp.where(in_far[j], damp[j] * kernel[j], 0.0),
                )
                for j in steps
            ]
            num = [dot(weight[j].astype(BF16), near_v[j], 1, 0) + damp[j] * state_num[j] for j in steps]
            inv = [
                1.0 / (jnp.sum(weight[j], axis=-1, keepdims=True) + damp[j] * state_den[j])
                for j in steps
            ]
            out = [num[j] * inv[j] for j in steps]
            for j in steps:
                hyb_ref[x_at[j][0], h, x_at[j][1]] = out[j].astype(BF16)
            t = [x_ref[x_at[j][0], 3, h, x_at[j][1]].astype(F32) for j in steps]
            d_out = [(out[j] - t[j]) * (2.0 / total_tokens) for j in steps]
            d_num = [d_out[j] * inv[j] for j in steps]
            d_den = [-jnp.sum(d_out[j] * out[j], axis=-1, keepdims=True) * inv[j] for j in steps]
            n_hi, n_lo = zip(*[split(d_num[j]) for j in steps])
            d_weight = [dot(n_hi[j], near_v[j], 1, 1) + d_den[j] for j in steps]
            d_state = [
                dot(n_hi[j], s_hi[j], 1, 1)
                + (dot(n_lo[j], s_hi[j], 1, 1) + dot(n_hi[j], s_lo[j], 1, 1))
                for j in steps
            ]
            far = [jnp.where(in_far[j], damp[j] * d_weight[j], 0.0).astype(BF16) for j in steps]
            d_phi = [
                dot(far[j], near_p[j], 1, 0) + damp[j] * (d_state[j] + d_den[j] * sums[j])
                for j in steps
            ]
            grad = [dot((damp[j] * d_num[j]).astype(BF16), phi[j], 0, 0) for j in steps]
            rate = [jnp.sum((damp[j] * d_den[j]) * phi32[j], axis=0, keepdims=True) for j in steps]
            for j in steps:
                grads[h, c[j]] = grad[j]
                rates[h, c[j]] = rate[j]
            first = i == 0
            all_grads[...] += jnp.where(first, 0.0, grad[0]) + sum(grad[1:])
            all_rates[...] += jnp.where(first, 0.0, rate[0]) + sum(rate[1:])
            d_near = [dot(far[j], phi[j], 0, 0) for j in steps]
            d_pad[h, at[0]] += d_near[0][:window]
            for j in steps[1:]:
                d_pad[h, at[j]] = d_near[j - 1][window:] + d_near[j][:window]
            last = pl.ds(pl.multiple_of((i * batch + batch) * window, window), window)
            d_pad[h, last] = d_near[-1][window:]
            for j in steps:
                d_q[h, at[j]] = d_phi[j]
            return carry

        lax.fori_loop(0, blocks // batch, forward, 0)

        a_hi, a_lo = split(all_grads[...])
        v_halo = halo_ref[1, h]
        send_ref[h, size + 8 :] = (
            d_pad[h, :window] + (dot(v_halo, a_hi, 1, 0) + dot(v_halo, a_lo, 1, 0)) + all_rates[...]
        )
        send_ref[h, :size] = all_grads[...] + grads[h, 0]
        send_ref[h, size : size + 1] = all_rates[...] + rates[h, 0]
        send_ref[h, size + 1 : size + 8] = jnp.zeros((7, size), F32)


def attend_call(x, halo, prior, live, map_k, phi_k, phi_q, total_tokens):
    chunks, _, heads, rows, size = x.shape
    tokens = chunks * rows
    blocks = tokens // WINDOW
    vmem = pltpu.VMEM
    shape = jax.ShapeDtypeStruct
    return resident(
        functools.partial(attend, total_tokens),
        [
            shape((chunks, heads, rows, size), BF16),
            shape((heads, size + 8 + WINDOW, size), F32),
            vmem((heads, tokens, size), F32),
            vmem((heads, tokens + WINDOW, size), F32),
            vmem((heads, blocks, size, size), F32),
            vmem((heads, blocks, 1, size), F32),
        ],
        [
            vmem((tokens + WINDOW, size), BF16),
            vmem((tokens + WINDOW, size), BF16),
            vmem((tokens + WINDOW, size), BF16),
            vmem((size, size), F32),
            vmem((1, size), F32),
            vmem((size, size), F32),
            vmem((1, size), F32),
        ],
        live,
        x,
        halo,
        prior,
        map_k,
        phi_k,
        phi_q,
        smem=1,
        name="attend",
    )


def sum_maps(x_ref, which, head, u_ref):
    chunks, _, _, rows, size = x_ref.shape
    sum_chunks = math.gcd(chunks, SUM_CHUNKS)
    length = sum_chunks * rows

    def total(i, carry):
        at = pl.ds(pl.multiple_of(i * length, length), length)
        mine = pl.ds(i * sum_chunks, sum_chunks)
        return carry + dot(u_ref[at], x_ref[mine, which, head].reshape(length, size), 0, 0)

    return lax.fori_loop(0, chunks // sum_chunks, total, jnp.zeros((size, size), F32))[: size // 2]


def local_grads(x_ref, soft_q, d_q, d_pad, grads, rates, grad_ref, d_k, u_q, tail, tail_sum):
    chunks, _, heads, rows, size = x_ref.shape
    window = WINDOW
    per = rows // window
    blocks = chunks * per
    ones = half_ones(size)
    back_batch = math.gcd(blocks, BACK_BLOCKS)
    grad_ref[...] = jnp.zeros_like(grad_ref)

    @over_heads(heads)
    def _(h):
        tail[...] = jnp.zeros_like(tail)
        tail_sum[...] = jnp.zeros_like(tail_sum)

        def backward(i, carry):
            steps = range(back_batch)
            c = [blocks - 1 - (i * back_batch + j) for j in steps]
            at = [pl.ds(pl.multiple_of(cj * window, window), window) for cj in c]
            after = [pl.ds(pl.multiple_of(cj * window + window, window), window) for cj in c]
            more = i > 0
            later = jnp.minimum(c[0] + 1, blocks - 1)
            tails = [tail[...], tail[...] + jnp.where(more, grads[h, later], 0.0)]
            tail_sums = [tail_sum[...], tail_sum[...] + jnp.where(more, rates[h, later], 0.0)]
            for j in steps[1:]:
                tails.append(tails[-1] + grads[h, c[j] + 1])
                tail_sums.append(tail_sums[-1] + rates[h, c[j] + 1])
            tail[...] = tails[-1]
            tail_sum[...] = tail_sums[-1]
            v = [
                x_ref[cj // per, 1, h, pl.ds(pl.multiple_of(cj % per * window, window), window)]
                for cj in c
            ]
            t_hi, t_lo = zip(*[split(tails[j]) for j in steps])
            for j in steps:
                d_k[h, at[j]] = (
                    d_pad[h, after[j]]
                    + (dot(v[j], t_hi[j], 1, 0) + dot(v[j], t_lo[j], 1, 0))
                    + tail_sums[j]
                )
            u = map_grad([soft_q[h, a] for a in at], [d_q[h, a] for a in at], ones)
            for j in steps:
                u_q[at[j]] = u[j]
            return carry

        lax.fori_loop(0, blocks // back_batch, backward, 0)
        grad_ref[...] += sum_maps(x_ref, 2, h, u_q)


def local_grads_call(x, soft_q, d_q, d_pad, grads, rates):
    chunks, _, heads, rows, size = x.shape
    tokens = chunks * rows
    return resident(
        local_grads,
        [pltpu.VMEM((size // 2, size), F32), pltpu.VMEM((heads, tokens, size), F32)],
        [
            pltpu.VMEM((tokens, size), BF16),
            pltpu.VMEM((size, size), F32),
            pltpu.VMEM((1, size), F32),
        ],
        x,
        soft_q,
        d_q,
        d_pad,
        grads,
        rates,
        name="local_grads",
    )


def key_grads(far, x_ref, soft_k, d_k, local_ref, got_ref, *refs):
    beyond_ref = refs[0] if far else None
    grad_ref, u_k = refs[-2:]
    chunks, _, heads, rows, size = x_ref.shape
    window = WINDOW
    half = size // 2
    ones = half_ones(size)
    batch = math.gcd(chunks, FEATURE_CHUNKS)
    grad_ref[:half] = local_ref[...]
    grad_ref[half:] = jnp.zeros((half, size), F32)

    @over_heads(heads)
    def _(h):
        states, sums = got_ref[h, :size], got_ref[h, size : size + 1]
        if far:
            b_hi, b_lo = split(beyond_ref[h, :size])
            b_sum = beyond_ref[h, size : size + 1]
            states, sums = states + beyond_ref[h, :size], sums + b_sum
        l_hi, l_lo = split(states)

        def features(i, carry):
            steps = range(batch)
            at = [pl.ds(pl.multiple_of((i * batch + j) * rows, rows), rows) for j in steps]
            d_phi = []
            for j in steps:
                v = x_ref[i * batch + j, 1, h]
                d_phi.append(d_k[h, at[j]] + (dot(v, l_hi, 1, 0) + dot(v, l_lo, 1, 0)) + sums)
            edge = d_k[h, at[-1]][rows - window :] + got_ref[h, size + 8 :]
            if far:
                v = x_ref[chunks - 1, 1, h, rows - window :]
                edge = edge + (dot(v, b_hi, 1, 0) + dot(v, b_lo, 1, 0)) + b_sum
            last = i == chunks // batch - 1
            d_phi[-1] = jnp.concatenate(
                [d_phi[-1][: rows - window], jnp.where(last, edge, d_phi[-1][rows - window :])], 0
            )
            u = map_grad([soft_k[h, a] for a in at], d_phi, ones)
            for j in steps:
                u_k[at[j]] = u[j]
            return carry

        lax.fori_loop(0, chunks // batch, features, 0)
        grad_ref[half:] += sum_maps(x_ref, 0, h, u_k)


def key_grads_call(x, soft_k, d_k, local, got, beyond):
    chunks, _, heads, rows, size = x.shape
    far = () if beyond is None else (beyond,)
    return resident(
        functools.partial(key_grads, bool(far)),
        [jax.ShapeDtypeStruct((size, size), F32)],
        [pltpu.VMEM((chunks * rows, size), BF16)],
        x,
        soft_k,
        d_k,
        local,
        got,
        *far,
        name="key_grads",
    )[0]


def deal(*refs):
    out_ref = refs[-1]
    groups, _, heads, rows, size = out_ref.shape
    for n, ref in enumerate(refs[:-1]):
        x = jnp.swapaxes(ref[...].astype(F32), 0, 1).astype(BF16)
        out_ref[:, n] = x.reshape(groups, heads, rows, size)


def deal_call(arrays, group):
    rows, heads, size = arrays[0].shape
    step = math.gcd(rows, DEAL_ROWS)
    own = heads // group
    return pl.pallas_call(
        deal,
        grid=(rows // step,),
        in_specs=[pl.BlockSpec((step, heads, size), lambda i: (i, 0, 0))] * len(arrays),
        out_specs=pl.BlockSpec((group, len(arrays), own, step, size), lambda i: (0, 0, 0, i, 0)),
        out_shape=jax.ShapeDtypeStruct((group, len(arrays), own, rows, size), BF16),
        name="deal",
    )(*arrays)


def sum_everywhere(value):
    for axis in ("head", "seq"):
        count = lax.axis_size(axis)
        if count & (count - 1):
            value = lax.psum(value, axis)
            continue
        bit = 1
        while bit < count:
            wide = 4 if 2 * bit < count else 2
            others = [
                lax.ppermute(value, axis, [(i, i ^ (m * bit)) for i in range(count)])
                for m in range(1, wide)
            ]
            value = value + others[0]
            if wide == 4:
                value = value + (others[1] + others[2])
            bit *= wide
    return value


def shift(array, steps):
    count = lax.axis_size("seq")
    pairs = [(i, i + steps) for i in range(count) if 0 <= i + steps < count]
    if not pairs:
        return jnp.zeros_like(array)
    return lax.ppermute(array, "seq", pairs)


def far_sum(array, group, groups, sign):
    if groups < 3:
        return None
    total = shift(array, sign * 2 * group)
    reach = 1
    while reach < groups - 2:
        total = total + shift(total, sign * reach * group)
        reach *= 2
    return total


def per_device(queries, keys, values, target, map_q, map_k):
    rows, heads, size = queries.shape
    seq_count = lax.axis_size("seq")
    here = lax.axis_index("seq")
    total_tokens = rows * seq_count
    group = math.gcd(seq_count, heads)
    if group == seq_count and group % 2 == 0:
        group //= 2
    groups = seq_count // group
    members = [list(range(g * group, (g + 1) * group)) for g in range(groups)]

    def trade(array):
        if group == 1:
            return array
        return lax.all_to_all(array, "seq", 0, 0, axis_index_groups=members)

    x = trade(deal_call((keys, values, queries, target), group))

    both_q = jnp.concatenate([map_q.T, -map_q.T], 0)
    both_k = jnp.concatenate([map_k.T, -map_k.T], 0)
    live = (here >= group).astype(jnp.int32).reshape(1)
    sums, last, halo = key_states_call(x, both_k)
    prior = shift(sums, group)
    halo = shift(halo, group)
    if groups > 2:
        prior = prior + far_sum(sums + last, group, groups, 1)
    soft_k, soft_q, phi_k, phi_q = feature_maps_call(x, both_k, both_q)
    hyb, send, d_q, d_pad, grads, rates = attend_call(
        x, halo, prior, live, both_k, phi_k, phi_q, total_tokens
    )
    got = shift(send, -group)
    beyond = far_sum(send, group, groups, -1)
    local, d_k = local_grads_call(x, soft_q, d_q, d_pad, grads, rates)
    hyb, local = lax.optimization_barrier((hyb, local))
    hybrid = trade(hyb).transpose(2, 0, 1, 3).reshape(rows, heads, size)
    grad = sum_everywhere(key_grads_call(x, soft_k, d_k, local, got, beyond))
    feat = map_q.shape[1]
    return hybrid, grad[:feat].T, grad[feat:].T


def solution(mesh):
    tokens = P("seq", "head", None)
    return jax.shard_map(
        per_device,
        mesh=mesh,
        in_specs=(tokens, tokens, tokens, tokens, P(), P()),
        out_specs=(tokens, P(), P()),
        check_vma=False,
    )
```
